32 devices in a mesh: occ: 8 (over z, x), aux: 4 (over y, core).
Axes of the slice: x: 2, y: 2, z: 4, core: 2. Of those that a mesh axis runs over, the one named last changes fastest.
Arguments:
- half_integrals: bfloat16 [8, 1024, 1024], P(None, 'aux'), may hold values from -1 to 1
- vir_coef: bfloat16 [1024, 768], P(None, 'occ'), may hold values from -0.1875 to 0.1875
- occ_energy: float32 [8], replicated, may hold values from -3 to -0.3
- vir_energy: float32 [768], replicated, may hold values from 0.1 to 2
Outputs:
- three_index: float32 [1024, 8, 768], P('aux', 'occ')
- vir_density: float32 [768, 768], P(('occ', 'aux'))
The draws below stay inside these ranges and needn't reach their ends.
All inputs are finite; a program needn't handle non-finite values.
Results may differ from the reference program's by a relative error of at most 0.0006.
The reference program's roundings to bfloat16 on the way (of `coupled` and `amplitude`) count: a program that leaves them out, or rounds other values in their place, can miss the bound.
Values may be sent and summed in bfloat16 or wider, within the bound.
A program may use at most 64 MiB of HBM per device.

```python
import jax
import jax.numpy as jnp
from jax import lax

NBF = 1024
NV = 768
NAUX = 1024
NO = 8


def draw_occ_energy(key, part):
    offsets = jnp.arange(NO, dtype=jnp.int32).astype(jnp.float32)
    jitter = jax.random.uniform(key, (NO,), jnp.float32)
    return -3.0 + 2.7 * (offsets + jitter) / NO


def draw_vir_energy(key, part):
    offsets = jnp.arange(NV, dtype=jnp.int32).astype(jnp.float32)
    jitter = jax.random.uniform(jax.random.fold_in(key, 7), (NV,), jnp.float32)
    return 0.1 + 1.9 * (offsets + jitter) / NV


def block_scale(own_key, extent, pieces, smallest, top_value):
    def one(position, blocks):
        steps = jax.random.uniform(jax.random.fold_in(jax.random.fold_in(own_key, 6), position), (blocks,), jnp.float32, smallest / len(pieces), top_value / len(pieces))
        return jnp.repeat(jnp.exp(steps), extent[position] // blocks).reshape((-1,) + (1,) * (len(extent) - position - 1))

    gain = one(*pieces[0])
    for cut in pieces[1:]:
        gain = gain * one(*cut)
    return gain


def centred(stream_key, extent, deviation, limit, split=(), kind=jnp.bfloat16):
    level = block_scale(stream_key, extent, split, -0.22, 0.18) if split else 1.0
    result = jax.random.normal(stream_key, extent, jnp.float32) * deviation * level
    return jnp.minimum(jnp.maximum(result, -limit), limit).astype(kind)


def setup_inputs(seed: int = 0) -> dict:
    arg_keys = jax.random.split(jax.random.key(seed), 5)
    half_integrals = centred(arg_keys[0], (NO, NAUX, NBF), (NAUX ** -0.25), 1.0, ((1, 4),))
    vir_coef = centred(arg_keys[1], (NBF, NV), NBF ** -0.5, 0.1875, ((1, 8),))
    occ_energy = draw_occ_energy(jax.random.fold_in(arg_keys[4], 71), 0)
    vir_energy = draw_vir_energy(jax.random.fold_in(arg_keys[4], 71), 0)
    return dict(half_integrals=half_integrals, vir_coef=vir_coef, occ_energy=occ_energy, vir_energy=vir_energy)


def reference(half_integrals, vir_coef, occ_energy, vir_energy):
    coupled = jnp.einsum('ipm,ma->iap', half_integrals.astype(jnp.float32), vir_coef.astype(jnp.float32)).astype(jnp.bfloat16)
    coupled = lax.optimization_barrier(coupled)
    spread = coupled.astype(jnp.float32)

    def one_orbital(density, orbital):
        own_rows = lax.dynamic_index_in_dim(spread, orbital, 0, keepdims=False)
        coulomb = jnp.einsum('jbp,ap->jba', spread, own_rows)
        denominator = occ_energy[orbital] + occ_energy[:, None, None] - vir_energy[None, :, None] - vir_energy[None, None, :]
        amplitude = (coulomb / denominator).astype(jnp.bfloat16)
        amplitude = lax.optimization_barrier(amplitude).astype(jnp.float32)
        gamma_rows = jnp.einsum('jba,jbp->pa', amplitude, spread)
        density = density + jnp.einsum('jca,jcd->ad', amplitude, amplitude)
        return density, gamma_rows

    density, stacked = lax.scan(one_orbital, jnp.zeros((NV, NV), jnp.float32), jnp.arange(NO, dtype=jnp.int32))
    three_index = jnp.transpose(stacked, (1, 0, 2))
    return three_index, density / (NO * NV)
```

```python
import functools

import jax
import jax.numpy as jnp
from jax import lax
from jax.experimental import pallas as pl
from jax.experimental.pallas import tpu as pltpu
from jax.sharding import PartitionSpec as P

MESH = pl.DeviceIdType.MESH
F32 = jnp.float32
LIMIT = 56 * 1024 * 1024


def remote(src, dst, send, recv, target):
    return pltpu.make_async_remote_copy(
        src_ref=src, dst_ref=dst, send_sem=send, recv_sem=recv, device_id=target, device_id_type=MESH
    )


def nearest_first(z, k, count):
    near = jnp.minimum(z, count - 1 - z)
    step = (k + 1) // 2
    both = z + step * (2 * (k % 2) - 1)
    low = z < count - 1 - z
    return jnp.where(k <= 2 * near, both, jnp.where(low, k, count - 1 - k))


def amplitude_kernel(n, aux, occ_e, own, row_e, col_e, three, vir, held, amps, sem_recv, sem_up, sem_down, sem_side, sem_own):
    o = lax.axis_index("occ")
    s = lax.axis_index("aux")
    z, low = o // 2, o % 2
    nz = n // 2
    virtuals, total = own.shape
    width = virtuals // aux
    above, below, side = o + 2, o - 2, 2 * z + 1 - low

    barrier = pltpu.get_barrier_semaphore()
    for peer in ((o + 2) % n, (o + n - 2) % n, side):
        pl.semaphore_signal(barrier, inc=1, device_id=(peer, s), device_id_type=MESH)

    def slot(index):
        return held.at[pl.ds(pl.multiple_of(index * width, width), width)]

    mine = own.at[pl.ds(pl.multiple_of(s * width, width), width)]
    local = pltpu.make_async_copy(mine, slot(o), sem_own)
    local.start()
    three[...] = jnp.zeros_like(three)
    vir[...] = jnp.zeros_like(vir)
    pl.semaphore_wait(barrier, 3)

    def sends(chain, src):
        block = 2 * chain + low
        up = remote(src, slot(block), sem_up.at[chain], sem_recv.at[block], (above, s))
        down = remote(src, slot(block), sem_down.at[chain], sem_recv.at[block], (below, s))
        across = remote(src, slot(block), sem_side.at[chain], sem_recv.at[block], (side, s))
        return (
            (jnp.logical_and(chain <= z, z < nz - 1), up),
            (jnp.logical_and(chain >= z, z > 0), down),
            (chain >= 0, across),
        )

    def each_send(chain, src, act):
        for allowed, copy in sends(chain, src):
            pl.when(allowed)(functools.partial(act, copy))

    each_send(z, mine, lambda copy: copy.start())

    def arrived(block):
        remote(slot(block), slot(block), sem_side.at[0], sem_recv.at[block], (side, s)).wait_recv()

    def absorb(block):
        rows = pl.ds(pl.multiple_of(block * width, width), width)
        coulomb = lax.dot_general(
            held[rows, :], own[...], (((1,), (1,)), ((), ())), preferred_element_type=F32
        )
        denominator = occ_e[o] + occ_e[block] - col_e[...] - row_e[...]
        amps[rows, :] = (coulomb / denominator).astype(jnp.bfloat16)

    def pair(chain):
        absorb(2 * chain + low)
        arrived(2 * chain + 1 - low)
        absorb(2 * chain + 1 - low)
        rows = pl.ds(pl.multiple_of(chain * 2 * width, 2 * width), 2 * width)
        contract = (((0,), (0,)), ((), ()))

        @pl.loop(0, virtuals // 256)
        def _(t):
            cols = pl.ds(pl.multiple_of(t * 256, 256), 256)
            vir[cols, :] += lax.dot_general(amps[rows, cols], amps[rows, :], contract, preferred_element_type=F32)

        @pl.loop(0, total // 256)
        def _(t):
            cols = pl.ds(pl.multiple_of(t * 256, 256), 256)
            three[cols, :] += lax.dot_general(held[rows, cols], amps[rows, :], contract, preferred_element_type=F32)

    local.wait()

    @pl.loop(1, nz)
    def _(k):
        chain = nearest_first(z, k, nz)
        arrived(2 * chain + low)
        each_send(chain, slot(2 * chain + low), lambda copy: copy.start())
        pair(nearest_first(z, k - 1, nz))

    pair(nearest_first(z, nz - 1, nz))

    @pl.loop(0, nz)
    def _(chain):
        each_send(chain, slot(2 * chain + low), lambda copy: copy.wait_send())


def reduce_kernel(
    n, nq, scale, three, vir, three_out, vir_out,
    t_pair, t_out, t_far, v_pair, v_sum, v_side, v_line, v_chain, v_col, v_far,
    pair_send, pair_recv, t_send, t_recv, vp_send, vp_recv, x_send, x_recv, z_send, z_recv, y_send, y_recv,
):
    o = lax.axis_index("occ")
    s = lax.axis_index("aux")
    q, c = s // 2, s % 2
    z, low = o // 2, o % 2
    nz = n // 2
    partner = (o, 2 * q + 1 - c)
    side = (2 * z + 1 - low, s)

    barrier = pltpu.get_barrier_semaphore()
    pl.semaphore_signal(barrier, inc=1, device_id=partner, device_id_type=MESH)
    pl.semaphore_signal(barrier, inc=1, device_id=side, device_id_type=MESH)
    for d in range(1, nq):
        pl.semaphore_signal(barrier, inc=1, device_id=(o, 2 * ((q + d) % nq) + c), device_id_type=MESH)
    for d in range(1, nz):
        pl.semaphore_signal(barrier, inc=1, device_id=(2 * ((z + d) % nz) + low, s), device_id_type=MESH)
    pl.semaphore_wait(barrier, nq + nz)

    v_swap = remote(vir.at[:, :, 1 - c], v_pair, vp_send, vp_recv, partner)
    v_swap.start()

    def swap(d):
        there = (q + d) % nq
        return remote(three.at[there, 1 - c], t_pair.at[d], pair_send.at[d], pair_recv.at[d], partner)

    def spread(d):
        return remote(t_out.at[d], t_far.at[d], t_send.at[d], t_recv.at[d], (o, 2 * ((q + d) % nq) + c))

    order = list(range(1, nq)) + [0]
    for d in order:
        swap(d).start()
    v_swap.wait()
    v_sum[...] = (vir[:, :, c] + v_pair[...]).reshape(v_sum.shape)
    x_swap = remote(v_sum.at[:, 1 - low], v_side, x_send, x_recv, side)
    x_swap.start()
    for d in order[:-1]:
        swap(d).wait()
        t_out[d] = three[(q + d) % nq, c] + t_pair[d]
        spread(d).start()
    swap(0).wait()
    three_out[...] = three[q, c] + t_pair[0]

    x_swap.wait()
    v_line[...] = v_sum[:, low] + v_side[...]

    def along(d):
        there = (z + d) % nz
        return remote(v_line.at[there], v_chain.at[d], z_send.at[d], z_recv.at[d], (2 * there + low, s))

    for d in range(1, nz):
        along(d).start()
    v_col[...] = v_line[z]
    for d in range(1, nz):
        along(d).wait()
        v_col[...] += v_chain[d]

    def between(d):
        there = (q + d) % nq
        return remote(v_col.at[there], v_far.at[d], y_send.at[d], y_recv.at[d], (o, 2 * there + c))

    for d in range(1, nq):
        between(d).start()
    for d in order[:-1]:
        spread(d).wait()
        three_out[...] += t_far[d]
    rows = v_col[q]
    for d in range(1, nq):
        between(d).wait()
        rows += v_far[d]
    vir_out[...] = rows / scale


def per_device(half_integrals, vir_coef, occ_energy, vir_energy):
    partial_block = jnp.einsum(
        "ipm,ma->iap", half_integrals, vir_coef, preferred_element_type=F32
    ).astype(jnp.bfloat16)
    local_block = lax.all_to_all(partial_block, "occ", split_axis=0, concat_axis=1, tiled=True)
    own = lax.all_gather(local_block, "aux", axis=2, tiled=True)[0]
    n, aux = lax.axis_size("occ"), lax.axis_size("aux")
    nz, nq = n // 2, aux // 2
    virtuals, total = own.shape
    width, tile, rows = virtuals // aux, total // aux, virtuals // (n * aux)
    row_e = vir_energy[None, :]
    col_e = lax.dynamic_slice_in_dim(vir_energy, lax.axis_index("aux") * width, width, 0)[:, None]
    vmem = pl.BlockSpec(memory_space=pltpu.VMEM)
    dma = pltpu.SemaphoreType.DMA
    three, vir = pl.pallas_call(
        functools.partial(amplitude_kernel, n, aux),
        out_shape=(
            jax.ShapeDtypeStruct((total, virtuals), F32),
            jax.ShapeDtypeStruct((virtuals, virtuals), F32),
        ),
        in_specs=[pl.BlockSpec(memory_space=pltpu.SMEM), vmem, vmem, vmem],
        out_specs=(vmem, vmem),
        scratch_shapes=[
            pltpu.VMEM((n * width, total), jnp.bfloat16),
            pltpu.VMEM((n * width, virtuals), jnp.bfloat16),
            dma((n,)), dma((nz,)), dma((nz,)), dma((nz,)), dma,
        ],
        compiler_params=pltpu.CompilerParams(
            collective_id=0, has_side_effects=True, vmem_limit_bytes=LIMIT
        ),
        name="amplitude",
    )(occ_energy, own, row_e, col_e)

    def room(*shape):
        return pltpu.VMEM(shape, F32)

    three_index, vir_rows = pl.pallas_call(
        functools.partial(reduce_kernel, n, nq, float(n * virtuals)),
        out_shape=(
            jax.ShapeDtypeStruct((tile, virtuals), F32),
            jax.ShapeDtypeStruct((rows, virtuals), F32),
        ),
        in_specs=[vmem, vmem],
        out_specs=(vmem, vmem),
        scratch_shapes=[
            room(nq, tile, virtuals), room(nq, tile, virtuals), room(nq, tile, virtuals),
            room(n, nq, rows, virtuals), room(nz, 2, nq, rows, virtuals),
            room(nz, nq, rows, virtuals), room(nz, nq, rows, virtuals), room(nz, nq, rows, virtuals),
            room(nq, rows, virtuals), room(nq, rows, virtuals),
            dma((nq,)), dma((nq,)), dma((nq,)), dma((nq,)), dma, dma, dma, dma,
            dma((nz,)), dma((nz,)), dma((nq,)), dma((nq,)),
        ],
        compiler_params=pltpu.CompilerParams(
            collective_id=1, has_side_effects=True, vmem_limit_bytes=LIMIT
        ),
        name="reduce",
    )(
        three.reshape(nq, 2, tile, virtuals),
        vir.reshape(n, nq, 2, rows, virtuals),
    )
    return three_index[:, None, :], vir_rows


def solution(mesh):
    return jax.shard_map(
        per_device,
        mesh=mesh,
        in_specs=(P(None, "aux", None), P(None, "occ"), P(), P()),
        out_specs=(P("aux", "occ", None), P(("occ", "aux"), None)),
        check_vma=False,
    )
```

```python
import functools

import jax
import jax.numpy as jnp
from jax import lax
from jax.experimental import pallas as pl
from jax.experimental.pallas import tpu as pltpu
from jax.sharding import PartitionSpec as P

MESH = pl.DeviceIdType.MESH
F32 = jnp.float32
LIMIT = 56 * 1024 * 1024


def remote(src, dst, send, recv, target):
    return pltpu.make_async_remote_copy(
        src_ref=src, dst_ref=dst, send_sem=send, recv_sem=recv, device_id=target, device_id_type=MESH
    )


def nearest_first(z, k, count):
    near = jnp.minimum(z, count - 1 - z)
    step = (k + 1) // 2
    both = z + step * (2 * (k % 2) - 1)
    low = z < count - 1 - z
    return jnp.where(k <= 2 * near, both, jnp.where(low, k, count - 1 - k))


def amplitude_kernel(
    n, nq, occ_e, half, coef, row_e, col_e, three, vir,
    ints, full, own, held, gift, amps,
    i_sem, c_copy, o_copy, c_recv, c_up, c_down, c_side, cp_send, cp_recv,
    own_send, own_recv, fw_send, fw_recv, pr_send, pr_recv, g_send, g_recv,
    h_recv, h_up, h_down, h_side,
):
    o = lax.axis_index("occ")
    s = lax.axis_index("aux")
    q, c = s // 2, s % 2
    z, low = o // 2, o % 2
    nz = n // 2
    width = amps.shape[0] // n
    part = coef.shape[1]
    cut = coef.shape[2]
    virtuals = amps.shape[1]
    above, below, side = o + 2, o - 2, 2 * z + 1 - low
    partner = (o, 2 * q + 1 - c)

    barrier = pltpu.get_barrier_semaphore()
    for peer in ((o + 2) % n, (o + n - 2) % n, side):
        pl.semaphore_signal(barrier, inc=1, device_id=(peer, s), device_id_type=MESH)
    pl.semaphore_signal(barrier, inc=1, device_id=partner, device_id_type=MESH)
    for d in range(1, nq):
        pl.semaphore_signal(barrier, inc=1, device_id=(o, 2 * ((q + d) % nq) + c), device_id_type=MESH)

    fetch = pltpu.make_async_copy(half, ints, i_sem)
    fetch.start()

    def span(index, size):
        return pl.ds(pl.multiple_of(index * size, size), size)

    keep = pltpu.make_async_copy(coef, full.at[:, span(o, part)], c_copy)
    keep.start()
    three[...] = jnp.zeros_like(three)
    vir[...] = jnp.zeros_like(vir)
    pl.semaphore_wait(barrier, 3 + nq)

    def relay(chain, src, dst, up, down, across, recv, act):
        pl.when(jnp.logical_and(chain <= z, z < nz - 1))(lambda: act(remote(src, dst, up, recv, (above, s))))
        pl.when(jnp.logical_and(chain >= z, z > 0))(lambda: act(remote(src, dst, down, recv, (below, s))))
        act(remote(src, dst, across, recv, (side, s)))

    def start(copy):
        copy.start()

    def sent(copy):
        copy.wait_send()

    def coef_slot(block):
        return full.at[c, span(block, part)]

    def coef_relay(chain, src, act):
        block = 2 * chain + low
        relay(chain, src, coef_slot(block), c_up.at[chain], c_down.at[chain], c_side.at[chain], c_recv.at[block], act)

    def coef_across(block):
        return remote(coef_slot(block), coef_slot(block), cp_send.at[block], cp_recv.at[block], partner)

    def coef_arrived(block):
        remote(coef_slot(block), coef_slot(block), c_side.at[0], c_recv.at[block], (side, s)).wait_recv()
        coef_across(block).start()

    coef_relay(z, coef.at[c], start)

    @pl.loop(1, nz)
    def _(k):
        chain = nearest_first(z, k, nz)
        block = 2 * chain + low
        remote(coef_slot(block), coef_slot(block), c_side.at[0], c_recv.at[block], (side, s)).wait_recv()
        coef_relay(chain, coef_slot(block), start)
        coef_across(block).start()
        coef_arrived(2 * nearest_first(z, k - 1, nz) + 1 - low)

    coef_arrived(2 * nearest_first(z, nz - 1, nz) + 1 - low)

    @pl.loop(1, n)
    def _(d):
        block = (o + d) % n
        other = full.at[1 - c, span(block, part)]
        remote(other, other, cp_send.at[block], cp_recv.at[block], partner).wait_recv()

    keep.wait()
    fetch.wait()

    def transform(block, rows):
        contract = (((1,), (1,)), ((), ()))
        return sum(
            lax.dot_general(
                full[h, rows, :], ints[block, :, h * cut : (h + 1) * cut], contract, preferred_element_type=F32
            )
            for h in range(2)
        ).astype(jnp.bfloat16)

    order = list(range(1, nq)) + [0]

    def chunk(there, core, group):
        return own.at[there, core, group]

    def to_partner(r):
        ref = chunk(q, c, (q + r) % nq)
        return remote(ref, ref, pr_send.at[r], pr_recv.at[r], partner)

    def to_chip(d, r):
        ref = chunk(q, c, (q + r) % nq)
        return remote(ref, ref, own_send.at[d, r], own_recv.at[d, r], (o, 2 * ((q + d) % nq) + c))

    def onward(d, r, core):
        there = (q + nq - d) % nq
        ref = chunk(there, core, (there + r) % nq)
        return remote(ref, ref, fw_send.at[d, r], fw_recv.at[d, r], partner)

    def from_chip(d, r):
        there = (q + nq - d) % nq
        ref = chunk(there, c, (there + r) % nq)
        remote(ref, ref, own_send.at[d, r], own_recv.at[d, r], partner).wait_recv()
        onward(d, r, c).start()

    for r in order:
        group = (q + r) % nq
        own[q, c, group] = transform(o, span(group, 2 * width))
        for d in range(1, nq):
            to_chip(d, r).start()
        to_partner(r).start()

    def give(block, core):
        return remote(
            gift.at[block], held.at[q, core, span(block, width)], g_send.at[block], g_recv.at[block], partner
        )

    @pl.loop(1, n)
    def _(d):
        block = (o + d) % n
        gift[block] = transform(block, span(2 * q + 1 - c, width))
        give(block, c).start()
        held[q, c, span(block, width), :] = transform(block, span(s, width))

    def held_slot(d, block):
        return held.at[(q + nq - d) % nq, :, span(block, width)]

    def own_slot(d):
        return own.at[(q + nq - d) % nq, :, q, span(c, width)]

    def held_relay(d, chain, src, act):
        block = 2 * chain + low
        relay(
            chain, src, held_slot(d, block), h_up.at[d, chain], h_down.at[d, chain], h_side.at[d, chain],
            h_recv.at[d, block], act,
        )

    def arrived(block):
        for d in range(1, nq):
            ref = held_slot(d, block)
            remote(ref, ref, h_side.at[d, 0], h_recv.at[d, block], (side, s)).wait_recv()

    for d in range(1, nq):
        from_chip(d, d)
    for d in range(1, nq):
        onward(d, d, 1 - c).wait_recv()
        held_relay(d, z, own_slot(d), start)
    rest = [(d, r) for d in range(1, nq) for r in order if r != d]
    for d, r in rest:
        from_chip(d, r)
    for r in order:
        ref = chunk(q, 1 - c, (q + r) % nq)
        remote(ref, ref, pr_send.at[r], pr_recv.at[r], partner).wait_recv()

    @pl.loop(1, n)
    def _(d):
        give((o + d) % n, 1 - c).wait_recv()

    for d, r in rest:
        onward(d, r, 1 - c).wait_recv()
    mine = pltpu.make_async_copy(
        own.at[:, :, q, span(c, width)], held.at[:, :, span(o, width)], o_copy
    )
    mine.start()
    mine.wait()

    def absorb(block):
        rows = span(block, width)
        coulomb = sum(
            lax.dot_general(
                held[t // 2, t % 2, rows, :], own[t // 2, t % 2].reshape(virtuals, -1),
                (((1,), (1,)), ((), ())), preferred_element_type=F32,
            )
            for t in range(2 * nq)
        )
        denominator = occ_e[o] + occ_e[block] - col_e[...] - row_e[...]
        amps[rows, :] = (coulomb / denominator).astype(jnp.bfloat16)

    def pair(chain):
        absorb(2 * chain + low)
        arrived(2 * chain + 1 - low)
        absorb(2 * chain + 1 - low)
        rows = span(chain, 2 * width)
        contract = (((0,), (0,)), ((), ()))

        @pl.loop(0, virtuals // 256)
        def _(t):
            cols = span(t, 256)
            vir[cols, :] += lax.dot_general(amps[rows, cols], amps[rows, :], contract, preferred_element_type=F32)

        @pl.loop(0, 2 * nq)
        def _(t):
            three[t // 2, t % 2] += lax.dot_general(
                held[t // 2, t % 2, rows, :], amps[rows, :], contract, preferred_element_type=F32
            )

    @pl.loop(1, nz)
    def _(k):
        chain = nearest_first(z, k, nz)
        arrived(2 * chain + low)
        for d in range(1, nq):
            held_relay(d, chain, held_slot(d, 2 * chain + low), start)
        pair(nearest_first(z, k - 1, nz))

    pair(nearest_first(z, nz - 1, nz))

    @pl.loop(0, nz)
    def _(chain):
        coef_relay(chain, coef_slot(2 * chain + low), sent)
        for d in range(1, nq):
            held_relay(d, chain, held_slot(d, 2 * chain + low), sent)

    @pl.loop(1, n)
    def _(d):
        block = (o + d) % n
        coef_across(block).wait_send()
        give(block, c).wait_send()

    for r in order:
        to_partner(r).wait_send()
        for d in range(1, nq):
            to_chip(d, r).wait_send()
            onward(d, r, c).wait_send()


def reduce_kernel(
    n, nq, three, vir, three_out, far_out, vir_out,
    t_pair, t_out, t_far, v_pair, v_sum, v_side, v_line, v_chain, v_col, v_far,
    pair_send, pair_recv, t_send, t_recv, vp_send, vp_recv, x_send, x_recv, z_send, z_recv, y_send, y_recv,
):
    o = lax.axis_index("occ")
    s = lax.axis_index("aux")
    q, c = s // 2, s % 2
    z, low = o // 2, o % 2
    nz = n // 2
    partner = (o, 2 * q + 1 - c)
    side = (2 * z + 1 - low, s)

    barrier = pltpu.get_barrier_semaphore()
    pl.semaphore_signal(barrier, inc=1, device_id=partner, device_id_type=MESH)
    pl.semaphore_signal(barrier, inc=1, device_id=side, device_id_type=MESH)
    for d in range(1, nq):
        pl.semaphore_signal(barrier, inc=1, device_id=(o, 2 * ((q + d) % nq) + c), device_id_type=MESH)
    for d in range(1, nz):
        pl.semaphore_signal(barrier, inc=1, device_id=(2 * ((z + d) % nz) + low, s), device_id_type=MESH)
    pl.semaphore_wait(barrier, nq + nz)

    v_swap = remote(vir.at[:, :, 1 - c], v_pair, vp_send, vp_recv, partner)
    v_swap.start()

    def swap(d):
        there = (q + d) % nq
        return remote(three.at[there, 1 - c], t_pair.at[d], pair_send.at[d], pair_recv.at[d], partner)

    def spread(d):
        return remote(t_out.at[d], t_far.at[d], t_send.at[d], t_recv.at[d], (o, 2 * ((q + d) % nq) + c))

    order = list(range(1, nq)) + [0]
    for d in order:
        swap(d).start()
    v_swap.wait()
    v_sum[...] = (vir[:, :, c] + v_pair[...]).reshape(v_sum.shape)
    x_swap = remote(v_sum.at[:, 1 - low], v_side, x_send, x_recv, side)
    x_swap.start()
    for d in order[:-1]:
        swap(d).wait()
        t_out[d] = three[(q + d) % nq, c] + t_pair[d]
        spread(d).start()
    swap(0).wait()
    three_out[...] = three[q, c] + t_pair[0]

    x_swap.wait()
    v_line[...] = v_sum[:, low] + v_side[...]

    def along(d):
        there = (z + d) % nz
        return remote(v_line.at[there], v_chain.at[d], z_send.at[d], z_recv.at[d], (2 * there + low, s))

    for d in range(1, nz):
        along(d).start()
    v_col[...] = v_line[z]
    for d in range(1, nz):
        along(d).wait()
        v_col[...] += v_chain[d]

    def between(d):
        there = (q + d) % nq
        return remote(v_col.at[there], v_far.at[d], y_send.at[d], y_recv.at[d], (o, 2 * there + c))

    for d in range(1, nq):
        between(d).start()
    for d in order[:-1]:
        spread(d).wait()
        far_out[...] = t_far[d] if d == 1 else far_out[...] + t_far[d]
    rows = v_col[q]
    for d in range(1, nq):
        between(d).wait()
        rows += v_far[d]
    vir_out[...] = rows


def per_device(half_integrals, vir_coef, occ_energy, vir_energy):
    n, aux = lax.axis_size("occ"), lax.axis_size("aux")
    nz, nq = n // 2, aux // 2
    _, tile, basis = half_integrals.shape
    part = vir_coef.shape[1]
    virtuals = part * n
    width, rows = virtuals // aux, virtuals // (n * aux)
    coef = vir_coef.reshape(2, basis // 2, part).transpose(0, 2, 1)
    row_e = vir_energy[None, :]
    col_e = lax.dynamic_slice_in_dim(vir_energy, lax.axis_index("aux") * width, width, 0)[:, None]
    vmem = pl.BlockSpec(memory_space=pltpu.VMEM)
    dma = pltpu.SemaphoreType.DMA
    half = jnp.bfloat16
    three, vir = pl.pallas_call(
        functools.partial(amplitude_kernel, n, nq),
        out_shape=(
            jax.ShapeDtypeStruct((nq, 2, tile, virtuals), F32),
            jax.ShapeDtypeStruct((virtuals, virtuals), F32),
        ),
        in_specs=[pl.BlockSpec(memory_space=pltpu.SMEM), pl.BlockSpec(memory_space=pl.ANY), vmem, vmem, vmem],
        out_specs=(vmem, vmem),
        scratch_shapes=[
            pltpu.VMEM(half_integrals.shape, half),
            pltpu.VMEM((2, virtuals, basis // 2), half),
            pltpu.VMEM((nq, 2, nq, 2 * width, tile), half),
            pltpu.VMEM((nq, 2, n * width, tile), half),
            pltpu.VMEM((n, width, tile), half),
            pltpu.VMEM((n * width, virtuals), half),
            dma, dma, dma, dma((n,)), dma((nz,)), dma((nz,)), dma((nz,)), dma((n,)), dma((n,)),
            dma((nq, nq)), dma((nq, nq)), dma((nq, nq)), dma((nq, nq)), dma((nq,)), dma((nq,)), dma((n,)), dma((n,)),
            dma((nq, n)), dma((nq, nz)), dma((nq, nz)), dma((nq, nz)),
        ],
        compiler_params=pltpu.CompilerParams(
            collective_id=0, has_side_effects=True, vmem_limit_bytes=LIMIT
        ),
        name="amplitude",
    )(occ_energy, half_integrals, coef, row_e, col_e)

    def room(*shape):
        return pltpu.VMEM(shape, F32)

    near, far, vir_rows = pl.pallas_call(
        functools.partial(reduce_kernel, n, nq),
        out_shape=(
            jax.ShapeDtypeStruct((tile, virtuals), F32),
            jax.ShapeDtypeStruct((tile, virtuals), F32),
            jax.ShapeDtypeStruct((rows, virtuals), F32),
        ),
        in_specs=[vmem, vmem],
        out_specs=(vmem, vmem, vmem),
        scratch_shapes=[
            room(nq, tile, virtuals), room(nq, tile, virtuals), room(nq, tile, virtuals),
            room(n, nq, rows, virtuals), room(nz, 2, nq, rows, virtuals),
            room(nz, nq, rows, virtuals), room(nz, nq, rows, virtuals), room(nz, nq, rows, virtuals),
            room(nq, rows, virtuals), room(nq, rows, virtuals),
            dma((nq,)), dma((nq,)), dma((nq,)), dma((nq,)), dma, dma, dma, dma,
            dma((nz,)), dma((nz,)), dma((nq,)), dma((nq,)),
        ],
        compiler_params=pltpu.CompilerParams(
            collective_id=1, has_side_effects=True, vmem_limit_bytes=LIMIT
        ),
        name="reduce",
    )(
        three,
        vir.reshape(n, nq, 2, rows, virtuals),
    )
    return (near + far)[:, None, :], vir_rows / (n * virtuals)


def solution(mesh):
    return jax.shard_map(
        per_device,
        mesh=mesh,
        in_specs=(P(None, "aux", None), P(None, "occ"), P(), P()),
        out_specs=(P("aux", "occ", None), P(("occ", "aux"), None)),
        check_vma=False,
    )
```

```python
import functools

import jax
import jax.numpy as jnp
from jax import lax
from jax.experimental import pallas as pl
from jax.experimental.pallas import tpu as pltpu
from jax.sharding import PartitionSpec as P

MESH = pl.DeviceIdType.MESH
F32 = jnp.float32
LIMIT = 56 * 1024 * 1024


def remote(src, dst, send, recv, target):
    return pltpu.make_async_remote_copy(
        src_ref=src, dst_ref=dst, send_sem=send, recv_sem=recv, device_id=target, device_id_type=MESH
    )


def nearest_first(z, k, count):
    near = jnp.minimum(z, count - 1 - z)
    step = (k + 1) // 2
    both = z + step * (2 * (k % 2) - 1)
    low = z < count - 1 - z
    return jnp.where(k <= 2 * near, both, jnp.where(low, k, count - 1 - k))


def greet(n, nq):
    o = lax.axis_index("occ")
    s = lax.axis_index("aux")
    q, c = s // 2, s % 2
    z, low = o // 2, o % 2
    nz = n // 2
    barrier = pltpu.get_barrier_semaphore()
    peers = [(2 * z + 1 - low, s), (o, 2 * q + 1 - c)]
    peers += [(o, 2 * ((q + d) % nq) + c) for d in range(1, nq)]
    peers += [(2 * ((z + d) % nz) + low, s) for d in range(1, nz)]
    for peer in peers:
        pl.semaphore_signal(barrier, inc=1, device_id=peer, device_id_type=MESH)
    return lambda: pl.semaphore_wait(barrier, len(peers))


def make_densities(
    n, nq, occ_e, half, coef, vir_e, three, vir,
    ints, full, own, held, gift, amps,
    i_sem, c_copy, o_copy, c_recv, c_up, c_down, c_side, cp_send, cp_recv,
    own_send, own_recv, fw_send, fw_recv, pr_send, pr_recv, g_send, g_recv,
    h_recv, h_up, h_down, h_side,
    vir_done=lambda: None,
):
    o = lax.axis_index("occ")
    s = lax.axis_index("aux")
    q, c = s // 2, s % 2
    z, low = o // 2, o % 2
    nz = n // 2
    width = amps.shape[0] // n
    part = coef.shape[0]
    cut = coef.shape[1] // 2
    virtuals = amps.shape[1]
    above, below, side = o + 2, o - 2, 2 * z + 1 - low
    partner = (o, 2 * q + 1 - c)
    entered = greet(n, nq)

    fetch = pltpu.make_async_copy(half, ints, i_sem)
    fetch.start()

    def span(index, size):
        return pl.ds(pl.multiple_of(index * size, size), size)

    def keep(h):
        return pltpu.make_async_copy(coef.at[:, h * cut : (h + 1) * cut], full.at[h, span(o, part)], c_copy.at[h])

    keep(0).start()
    keep(1).start()
    entered()

    def relay(chain, src, dst, up, down, across, recv, act):
        pl.when(jnp.logical_and(chain <= z, z < nz - 1))(lambda: act(remote(src, dst, up, recv, (above, s))))
        pl.when(jnp.logical_and(chain >= z, z > 0))(lambda: act(remote(src, dst, down, recv, (below, s))))
        act(remote(src, dst, across, recv, (side, s)))

    def start(copy):
        copy.start()

    def sent(copy):
        copy.wait_send()

    def coef_slot(block):
        return full.at[c, span(block, part)]

    def coef_relay(chain, src, act):
        block = 2 * chain + low
        relay(chain, src, coef_slot(block), c_up.at[chain], c_down.at[chain], c_side.at[chain], c_recv.at[block], act)

    def coef_across(block):
        return remote(coef_slot(block), coef_slot(block), cp_send.at[block], cp_recv.at[block], partner)

    def coef_arrived(block):
        remote(coef_slot(block), coef_slot(block), c_side.at[0], c_recv.at[block], (side, s)).wait_recv()
        coef_across(block).start()

    coef_relay(z, coef.at[:, span(c, cut)], start)
    three[...] = jnp.zeros_like(three)
    vir[...] = jnp.zeros_like(vir)
    row_e = vir_e[...].reshape(1, virtuals)
    here = lax.broadcasted_iota(jnp.int32, (width, virtuals), 0) + s * width
    there = lax.broadcasted_iota(jnp.int32, (width, virtuals), 1)
    col_e = jnp.sum(jnp.where(here == there, row_e, 0.0), axis=1, keepdims=True)

    @pl.loop(1, nz)
    def _(k):
        chain = nearest_first(z, k, nz)
        block = 2 * chain + low
        remote(coef_slot(block), coef_slot(block), c_side.at[0], c_recv.at[block], (side, s)).wait_recv()
        coef_relay(chain, coef_slot(block), start)
        coef_across(block).start()
        coef_arrived(2 * nearest_first(z, k - 1, nz) + 1 - low)

    coef_arrived(2 * nearest_first(z, nz - 1, nz) + 1 - low)

    @pl.loop(1, n)
    def _(d):
        block = (o + d) % n
        other = full.at[1 - c, span(block, part)]
        remote(other, other, cp_send.at[block], cp_recv.at[block], partner).wait_recv()

    keep(0).wait()
    keep(1).wait()
    fetch.wait()

    def transform(block, rows):
        contract = (((1,), (1,)), ((), ()))
        return sum(
            lax.dot_general(
                full[h, rows, :], ints[block, :, h * cut : (h + 1) * cut], contract, preferred_element_type=F32
            )
            for h in range(2)
        ).astype(jnp.bfloat16)

    order = list(range(1, nq)) + [0]

    def chunk(there, core, group):
        return own.at[there, core, group]

    def to_partner(r):
        ref = chunk(q, c, (q + r) % nq)
        return remote(ref, ref, pr_send.at[r], pr_recv.at[r], partner)

    def to_chip(d, r):
        ref = chunk(q, c, (q + r) % nq)
        return remote(ref, ref, own_send.at[d, r], own_recv.at[d, r], (o, 2 * ((q + d) % nq) + c))

    def onward(d, r, core):
        there = (q + nq - d) % nq
        ref = chunk(there, core, (there + r) % nq)
        return remote(ref, ref, fw_send.at[d, r], fw_recv.at[d, r], partner)

    def from_chip(d, r):
        there = (q + nq - d) % nq
        ref = chunk(there, c, (there + r) % nq)
        remote(ref, ref, own_send.at[d, r], own_recv.at[d, r], partner).wait_recv()
        onward(d, r, c).start()

    for r in order:
        group = (q + r) % nq
        own[q, c, group] = transform(o, span(group, 2 * width))
        for d in range(1, nq):
            to_chip(d, r).start()
        to_partner(r).start()

    def give(block, core):
        return remote(
            gift.at[block], held.at[q, core, span(block, width)], g_send.at[block], g_recv.at[block], partner
        )

    @pl.loop(1, n)
    def _(d):
        block = (o + d) % n
        gift[block] = transform(block, span(2 * q + 1 - c, width))
        give(block, c).start()
        held[q, c, span(block, width), :] = transform(block, span(s, width))

    def held_slot(d, block):
        return held.at[(q + nq - d) % nq, :, span(block, width)]

    def own_slot(d):
        return own.at[(q + nq - d) % nq, :, q, span(c, width)]

    def held_relay(d, chain, src, act):
        block = 2 * chain + low
        relay(
            chain, src, held_slot(d, block), h_up.at[d, chain], h_down.at[d, chain], h_side.at[d, chain],
            h_recv.at[d, block], act,
        )

    def arrived(block):
        for d in range(1, nq):
            ref = held_slot(d, block)
            remote(ref, ref, h_side.at[d, 0], h_recv.at[d, block], (side, s)).wait_recv()

    for d in range(1, nq):
        from_chip(d, d)
    for d in range(1, nq):
        onward(d, d, 1 - c).wait_recv()
        held_relay(d, z, own_slot(d), start)
    rest = [(d, r) for d in range(1, nq) for r in order if r != d]
    for d, r in rest:
        from_chip(d, r)
    for r in order:
        ref = chunk(q, 1 - c, (q + r) % nq)
        remote(ref, ref, pr_send.at[r], pr_recv.at[r], partner).wait_recv()

    @pl.loop(1, n)
    def _(d):
        give((o + d) % n, 1 - c).wait_recv()

    for d, r in rest:
        onward(d, r, 1 - c).wait_recv()
    mine = pltpu.make_async_copy(
        own.at[:, :, q, span(c, width)], held.at[:, :, span(o, width)], o_copy
    )
    mine.start()
    mine.wait()

    def absorb(block):
        rows = span(block, width)
        coulomb = sum(
            lax.dot_general(
                held[t // 2, t % 2, rows, :], own[t // 2, t % 2].reshape(virtuals, -1),
                (((1,), (1,)), ((), ())), preferred_element_type=F32,
            )
            for t in range(2 * nq)
        )
        denominator = occ_e[o] + occ_e[block] - col_e - row_e
        amps[rows, :] = (coulomb / denominator).astype(jnp.bfloat16)

    contract = (((0,), (0,)), ((), ()))
    piece = virtuals // 2 if len(vir.shape) > 2 else 256

    def add_vir(chain):
        rows = span(chain, 2 * width)

        @pl.loop(0, virtuals // piece)
        def _(t):
            new = lax.dot_general(
                amps[rows, span(t, piece)], amps[rows, :], contract, preferred_element_type=F32
            )
            where = span(t, vir.shape[0] * piece // virtuals)
            vir[where] += new.reshape((-1,) + vir.shape[1:])

    def add_three(chain):
        rows = span(chain, 2 * width)

        @pl.loop(0, 2 * nq)
        def _(t):
            three[t // 2, t % 2] += lax.dot_general(
                held[t // 2, t % 2, rows, :], amps[rows, :], contract, preferred_element_type=F32
            )

    def both(chain):
        absorb(2 * chain + low)
        arrived(2 * chain + 1 - low)
        absorb(2 * chain + 1 - low)

    @pl.loop(1, nz)
    def _(k):
        chain = nearest_first(z, k, nz)
        arrived(2 * chain + low)
        for d in range(1, nq):
            held_relay(d, chain, held_slot(d, 2 * chain + low), start)
        before = nearest_first(z, k - 1, nz)
        both(before)
        add_vir(before)
        add_three(before)

    last = nearest_first(z, nz - 1, nz)
    both(last)
    add_vir(last)
    vir_done()
    add_three(last)

    def finish():
        @pl.loop(0, nz)
        def _(chain):
            coef_relay(chain, coef_slot(2 * chain + low), sent)
            for d in range(1, nq):
                held_relay(d, chain, held_slot(d, 2 * chain + low), sent)

        @pl.loop(1, n)
        def _(d):
            block = (o + d) % n
            coef_across(block).wait_send()
            give(block, c).wait_send()

        for r in order:
            to_partner(r).wait_send()
            for d in range(1, nq):
                to_chip(d, r).wait_send()
                onward(d, r, c).wait_send()

    return finish


def reduction(
    n, nq, three, vir, near_out, far_out, vir_out,
    t_pair, t_out, t_far, v_pair, v_sum, v_side, v_line, v_chain, v_col, v_far,
    pair_send, pair_recv, t_send, t_recv, vp_send, vp_recv, x_send, x_recv, z_send, z_recv, y_send, y_recv,
):
    o = lax.axis_index("occ")
    s = lax.axis_index("aux")
    q, c = s // 2, s % 2
    z, low = o // 2, o % 2
    nz = n // 2
    chunks, chunk = v_pair.shape[0], v_pair.shape[-1]
    partner = (o, 2 * q + 1 - c)
    side = (2 * z + 1 - low, s)

    def cols(k):
        return pl.ds(k * chunk, chunk)

    def v_swap(k):
        return remote(vir.at[:, :, 1 - c, :, cols(k)], v_pair.at[k], vp_send.at[k], vp_recv.at[k], partner)

    def x_swap(k):
        return remote(v_sum.at[k, :, 1 - low], v_side.at[k], x_send.at[k], x_recv.at[k], side)

    def along(k, d):
        there = (z + d) % nz
        return remote(
            v_line.at[k, there], v_chain.at[k, d], z_send.at[k, d], z_recv.at[k, d], (2 * there + low, s)
        )

    def between(k, d):
        there = (q + d) % nq
        return remote(v_col.at[k, there], v_far.at[k, d], y_send.at[k, d], y_recv.at[k, d], (o, 2 * there + c))

    def swap(d):
        return remote(three.at[(q + d) % nq, 1 - c], t_pair.at[d], pair_send.at[d], pair_recv.at[d], partner)

    def spread(d):
        return remote(t_out.at[d], t_far.at[d], t_send.at[d], t_recv.at[d], (o, 2 * ((q + d) % nq) + c))

    order = list(range(1, nq)) + [0]

    def open_vir():
        for k in range(chunks):
            v_swap(k).start()

    def close():
        for d in order:
            swap(d).start()
        for k in range(chunks):
            v_swap(k).wait()
            v_sum[k] = (vir[:, :, c, :, cols(k)] + v_pair[k]).reshape(v_sum.shape[1:])
            x_swap(k).start()
        for d in order[:-1]:
            swap(d).wait()
            t_out[d] = three[(q + d) % nq, c] + t_pair[d]
            spread(d).start()
        for k in range(chunks):
            x_swap(k).wait()
            v_line[k] = v_sum[k, :, low] + v_side[k]
            for d in range(1, nz):
                along(k, d).start()
            if k == 0:
                swap(0).wait()
                near_out[...] = three[q, c] + t_pair[0]
        for k in range(chunks):
            held = v_line[k, z]
            for d in range(1, nz):
                along(k, d).wait()
                held += v_chain[k, d]
            v_col[k] = held
            for d in range(1, nq):
                between(k, d).start()
        for d in order[:-1]:
            spread(d).wait()
            far_out[...] = t_far[d] if d == 1 else far_out[...] + t_far[d]
        for k in range(chunks):
            rows = v_col[k, q]
            for d in range(1, nq):
                between(k, d).wait()
                rows += v_far[k, d]
            vir_out[:, cols(k)] = rows

    return open_vir, close


def amplitude_kernel(n, nq, *refs):
    make_densities(n, nq, *refs)()


def reduce_kernel(n, nq, *refs):
    greet(n, nq)()
    open_vir, close = reduction(n, nq, *refs)
    open_vir()
    close()


def whole_kernel(n, nq, inputs, outputs, count, *refs):
    operands, results, scratch = refs[:inputs], refs[inputs : inputs + outputs], refs[inputs + outputs :]
    three, vir, rest = scratch[0], scratch[1], scratch[2:]
    open_vir, close = reduction(n, nq, three, vir, *results, *rest[count:])
    finish = make_densities(n, nq, *operands, three, vir, *rest[:count], vir_done=open_vir)
    close()
    finish()


def per_device(half_integrals, vir_coef, occ_energy, vir_energy):
    n, aux = lax.axis_size("occ"), lax.axis_size("aux")
    nz, nq = n // 2, aux // 2
    _, tile, basis = half_integrals.shape
    part = vir_coef.shape[1]
    virtuals = part * n
    width, rows = virtuals // aux, virtuals // (n * aux)
    vmem = pl.BlockSpec(memory_space=pltpu.VMEM)
    dma = pltpu.SemaphoreType.DMA
    half = jnp.bfloat16
    chunks = virtuals // 256

    def room(*shape):
        return pltpu.VMEM(shape, F32)

    def result(*shape):
        return jax.ShapeDtypeStruct(shape, F32)

    def call(kernel, name, number, in_specs, out_shape, scratch, operands):
        return pl.pallas_call(
            kernel,
            out_shape=out_shape,
            in_specs=in_specs,
            out_specs=(vmem,) * len(out_shape),
            scratch_shapes=scratch,
            compiler_params=pltpu.CompilerParams(
                collective_id=number, has_side_effects=True, vmem_limit_bytes=LIMIT
            ),
            name=name,
        )(*operands)

    operands = (occ_energy, half_integrals, vir_coef.T, vir_energy)
    specs = [pl.BlockSpec(memory_space=pltpu.SMEM), pl.BlockSpec(memory_space=pl.ANY), vmem, vmem]
    make_scratch = [
        pltpu.VMEM(half_integrals.shape, half),
        pltpu.VMEM((2, virtuals, basis // 2), half),
        pltpu.VMEM((nq, 2, nq, 2 * width, tile), half),
        pltpu.VMEM((nq, 2, n * width, tile), half),
        pltpu.VMEM((n, width, tile), half),
        pltpu.VMEM((n * width, virtuals), half),
        dma, dma((2,)), dma, dma((n,)), dma((nz,)), dma((nz,)), dma((nz,)), dma((n,)), dma((n,)),
        dma((nq, nq)), dma((nq, nq)), dma((nq, nq)), dma((nq, nq)), dma((nq,)), dma((nq,)), dma((n,)), dma((n,)),
        dma((nq, n)), dma((nq, nz)), dma((nq, nz)), dma((nq, nz)),
    ]
    reduce_scratch = [
        room(nq, tile, virtuals), room(nq, tile, virtuals), room(nq, tile, virtuals),
        room(chunks, n, nq, rows, 256), room(chunks, nz, 2, nq, rows, 256),
        room(chunks, nz, nq, rows, 256), room(chunks, nz, nq, rows, 256), room(chunks, nz, nq, rows, 256),
        room(chunks, nq, rows, 256), room(chunks, nq, rows, 256),
        dma((nq,)), dma((nq,)), dma((nq,)), dma((nq,)), dma((chunks,)), dma((chunks,)), dma((chunks,)), dma((chunks,)),
        dma((chunks, nz)), dma((chunks, nz)), dma((chunks, nq)), dma((chunks, nq)),
    ]
    sums = (nq, 2, tile, virtuals)
    groups = (n, nq, 2, rows, virtuals)
    finals = (result(tile, virtuals), result(tile, virtuals), result(rows, virtuals))
    if rows % 8 == 0:
        kernel = functools.partial(whole_kernel, n, nq, len(specs), len(finals), len(make_scratch))
        scratch = [room(*sums), room(*groups)] + make_scratch + reduce_scratch
        near, far, vir_rows = call(kernel, "densities", 0, specs, finals, scratch, operands)
    else:
        kernel = functools.partial(amplitude_kernel, n, nq)
        partials = (result(*sums), result(virtuals, virtuals))
        three, vir = call(kernel, "amplitude", 0, specs, partials, make_scratch, operands)
        kernel = functools.partial(reduce_kernel, n, nq)
        near, far, vir_rows = call(
            kernel, "reduce", 1, [vmem, vmem], finals, reduce_scratch, (three, vir.reshape(groups))
        )
    return (near + far)[:, None, :], vir_rows / (n * virtuals)


def solution(mesh):
    return jax.shard_map(
        per_device,
        mesh=mesh,
        in_specs=(P(None, "aux", None), P(None, "occ"), P(), P()),
        out_specs=(P("aux", "occ", None), P(("occ", "aux"), None)),
        check_vma=False,
    )
```

```python
import functools

import jax
import jax.numpy as jnp
from jax import lax
from jax.experimental import pallas as pl
from jax.experimental.pallas import tpu as pltpu
from jax.sharding import PartitionSpec as P

MESH = pl.DeviceIdType.MESH
F32 = jnp.float32
LIMIT = 56 * 1024 * 1024


def remote(src, dst, send, recv, target):
    return pltpu.make_async_remote_copy(
        src_ref=src, dst_ref=dst, send_sem=send, recv_sem=recv, device_id=target, device_id_type=MESH
    )


def nearest_first(z, k, count):
    near = jnp.minimum(z, count - 1 - z)
    step = (k + 1) // 2
    both = z + step * (2 * (k % 2) - 1)
    low = z < count - 1 - z
    return jnp.where(k <= 2 * near, both, jnp.where(low, k, count - 1 - k))


def greet(n, nq):
    o = lax.axis_index("occ")
    s = lax.axis_index("aux")
    q, c = s // 2, s % 2
    z, low = o // 2, o % 2
    nz = n // 2
    barrier = pltpu.get_barrier_semaphore()
    peers = [(2 * z + 1 - low, s), (o, 2 * q + 1 - c)]
    peers += [(o, 2 * ((q + d) % nq) + c) for d in range(1, nq)]
    peers += [(2 * ((z + d) % nz) + low, s) for d in range(1, nz)]
    for peer in peers:
        pl.semaphore_signal(barrier, inc=1, device_id=peer, device_id_type=MESH)
    return lambda: pl.semaphore_wait(barrier, len(peers))


def make_densities(
    n, nq, occ_e, half, coef, vir_e, three, vir,
    ints, full, own, held, gift, amps,
    i_sem, c_copy, o_copy, c_recv, c_up, c_down, c_side, cp_send, cp_recv,
    own_send, own_recv, fw_send, fw_recv, pr_send, pr_recv, g_send, g_recv,
    h_recv, h_up, h_down, h_side,
    vir_done=lambda: None,
):
    o = lax.axis_index("occ")
    s = lax.axis_index("aux")
    q, c = s // 2, s % 2
    z, low = o // 2, o % 2
    nz = n // 2
    width = amps.shape[0] // n
    part = coef.shape[0]
    cut = coef.shape[1] // 2
    virtuals = amps.shape[1]
    above, below, side = o + 2, o - 2, 2 * z + 1 - low
    partner = (o, 2 * q + 1 - c)
    entered = greet(n, nq)

    fetch = pltpu.make_async_copy(half, ints, i_sem)
    fetch.start()

    def span(index, size):
        return pl.ds(pl.multiple_of(index * size, size), size)

    def keep(h):
        return pltpu.make_async_copy(coef.at[:, h * cut : (h + 1) * cut], full.at[h, span(o, part)], c_copy.at[h])

    keep(0).start()
    keep(1).start()
    entered()

    def relay(chain, src, dst, up, down, across, recv, act):
        pl.when(jnp.logical_and(chain <= z, z < nz - 1))(lambda: act(remote(src, dst, up, recv, (above, s))))
        pl.when(jnp.logical_and(chain >= z, z > 0))(lambda: act(remote(src, dst, down, recv, (below, s))))
        act(remote(src, dst, across, recv, (side, s)))

    def start(copy):
        copy.start()

    def sent(copy):
        copy.wait_send()

    def coef_slot(block):
        return full.at[c, span(block, part)]

    def coef_relay(chain, src, act):
        block = 2 * chain + low
        relay(chain, src, coef_slot(block), c_up.at[chain], c_down.at[chain], c_side.at[chain], c_recv.at[block], act)

    def coef_across(block):
        return remote(coef_slot(block), coef_slot(block), cp_send.at[block], cp_recv.at[block], partner)

    def coef_arrived(block):
        remote(coef_slot(block), coef_slot(block), c_side.at[0], c_recv.at[block], (side, s)).wait_recv()
        coef_across(block).start()

    coef_relay(z, coef.at[:, span(c, cut)], start)
    three[...] = jnp.zeros_like(three)
    vir[...] = jnp.zeros_like(vir)
    row_e = vir_e[...].reshape(1, virtuals)
    here = lax.broadcasted_iota(jnp.int32, (width, virtuals), 0) + s * width
    there = lax.broadcasted_iota(jnp.int32, (width, virtuals), 1)
    col_e = jnp.sum(jnp.where(here == there, row_e, 0.0), axis=1, keepdims=True)

    @pl.loop(1, nz)
    def _(k):
        chain = nearest_first(z, k, nz)
        block = 2 * chain + low
        remote(coef_slot(block), coef_slot(block), c_side.at[0], c_recv.at[block], (side, s)).wait_recv()
        coef_relay(chain, coef_slot(block), start)
        coef_across(block).start()
        coef_arrived(2 * nearest_first(z, k - 1, nz) + 1 - low)

    coef_arrived(2 * nearest_first(z, nz - 1, nz) + 1 - low)

    @pl.loop(1, n)
    def _(d):
        block = (o + d) % n
        other = full.at[1 - c, span(block, part)]
        remote(other, other, cp_send.at[block], cp_recv.at[block], partner).wait_recv()

    keep(0).wait()
    keep(1).wait()
    fetch.wait()

    def transform(block, rows):
        contract = (((1,), (1,)), ((), ()))
        return sum(
            lax.dot_general(
                full[h, rows, :], ints[block, :, h * cut : (h + 1) * cut], contract, preferred_element_type=F32
            )
            for h in range(2)
        ).astype(jnp.bfloat16)

    order = list(range(1, nq)) + [0]

    def chunk(there, core, group):
        return own.at[there, core, group]

    def to_partner(r):
        ref = chunk(q, c, (q + r) % nq)
        return remote(ref, ref, pr_send.at[r], pr_recv.at[r], partner)

    def to_chip(d, r):
        ref = chunk(q, c, (q + r) % nq)
        return remote(ref, ref, own_send.at[d, r], own_recv.at[d, r], (o, 2 * ((q + d) % nq) + c))

    def onward(d, r, core):
        there = (q + nq - d) % nq
        ref = chunk(there, core, (there + r) % nq)
        return remote(ref, ref, fw_send.at[d, r], fw_recv.at[d, r], partner)

    def from_chip(d, r):
        there = (q + nq - d) % nq
        ref = chunk(there, c, (there + r) % nq)
        remote(ref, ref, own_send.at[d, r], own_recv.at[d, r], partner).wait_recv()
        onward(d, r, c).start()

    for r in order:
        group = (q + r) % nq
        own[q, c, group] = transform(o, span(group, 2 * width))
        for d in range(1, nq):
            to_chip(d, r).start()
        to_partner(r).start()

    def give(block, core):
        return remote(
            gift.at[block], held.at[q, core, span(block, width)], g_send.at[block], g_recv.at[block], partner
        )

    @pl.loop(1, n)
    def _(d):
        block = (o + d) % n
        gift[block] = transform(block, span(2 * q + 1 - c, width))
        give(block, c).start()
        held[q, c, span(block, width), :] = transform(block, span(s, width))

    def held_slot(d, block):
        return held.at[(q + nq - d) % nq, :, span(block, width)]

    def own_slot(d):
        return own.at[(q + nq - d) % nq, :, q, span(c, width)]

    def held_relay(d, chain, src, act):
        block = 2 * chain + low
        relay(
            chain, src, held_slot(d, block), h_up.at[d, chain], h_down.at[d, chain], h_side.at[d, chain],
            h_recv.at[d, block], act,
        )

    def arrived(block):
        for d in range(1, nq):
            ref = held_slot(d, block)
            remote(ref, ref, h_side.at[d, 0], h_recv.at[d, block], (side, s)).wait_recv()

    for d in range(1, nq):
        from_chip(d, d)
    for d in range(1, nq):
        onward(d, d, 1 - c).wait_recv()
        held_relay(d, z, own_slot(d), start)
    rest = [(d, r) for d in range(1, nq) for r in order if r != d]
    for d, r in rest:
        from_chip(d, r)
    for r in order:
        ref = chunk(q, 1 - c, (q + r) % nq)
        remote(ref, ref, pr_send.at[r], pr_recv.at[r], partner).wait_recv()

    @pl.loop(1, n)
    def _(d):
        give((o + d) % n, 1 - c).wait_recv()

    for d, r in rest:
        onward(d, r, 1 - c).wait_recv()
    mine = pltpu.make_async_copy(
        own.at[:, :, q, span(c, width)], held.at[:, :, span(o, width)], o_copy
    )
    mine.start()
    mine.wait()

    def absorb(block):
        rows = span(block, width)
        coulomb = sum(
            lax.dot_general(
                held[t // 2, t % 2, rows, :], own[t // 2, t % 2].reshape(virtuals, -1),
                (((1,), (1,)), ((), ())), preferred_element_type=F32,
            )
            for t in range(2 * nq)
        )
        denominator = occ_e[o] + occ_e[block] - col_e - row_e
        amps[rows, :] = (coulomb / denominator).astype(jnp.bfloat16)

    contract = (((0,), (0,)), ((), ()))
    piece = virtuals // 2 if len(vir.shape) > 2 else 256

    def add_vir(chain):
        rows = span(chain, 2 * width)

        @pl.loop(0, virtuals // piece)
        def _(t):
            new = lax.dot_general(
                amps[rows, span(t, piece)], amps[rows, :], contract, preferred_element_type=F32
            )
            where = span(t, vir.shape[0] * piece // virtuals)
            vir[where] += new.reshape((-1,) + vir.shape[1:])

    def add_three(chain):
        rows = span(chain, 2 * width)

        @pl.loop(0, 2 * nq)
        def _(t):
            three[t // 2, t % 2] += lax.dot_general(
                held[t // 2, t % 2, rows, :], amps[rows, :], contract, preferred_element_type=F32
            )

    def both(chain):
        absorb(2 * chain + low)
        arrived(2 * chain + 1 - low)
        absorb(2 * chain + 1 - low)

    @pl.loop(1, nz)
    def _(k):
        chain = nearest_first(z, k, nz)
        arrived(2 * chain + low)
        for d in range(1, nq):
            held_relay(d, chain, held_slot(d, 2 * chain + low), start)
        before = nearest_first(z, k - 1, nz)
        both(before)
        add_vir(before)
        add_three(before)

    last = nearest_first(z, nz - 1, nz)
    both(last)
    add_vir(last)
    vir_done()
    add_three(last)

    def finish():
        @pl.loop(0, nz)
        def _(chain):
            coef_relay(chain, coef_slot(2 * chain + low), sent)
            for d in range(1, nq):
                held_relay(d, chain, held_slot(d, 2 * chain + low), sent)

        @pl.loop(1, n)
        def _(d):
            block = (o + d) % n
            coef_across(block).wait_send()
            give(block, c).wait_send()

        for r in order:
            to_partner(r).wait_send()
            for d in range(1, nq):
                to_chip(d, r).wait_send()
                onward(d, r, c).wait_send()

    return finish


def reduction(
    n, nq, three, vir, near_out, far_out, vir_out,
    t_pair, t_out, t_far, v_pair, v_sum, v_side, v_line, v_chain, v_col, v_far,
    pair_send, pair_recv, t_send, t_recv, vp_send, vp_recv, x_send, x_recv, z_send, z_recv, y_send, y_recv,
):
    o = lax.axis_index("occ")
    s = lax.axis_index("aux")
    q, c = s // 2, s % 2
    z, low = o // 2, o % 2
    nz = n // 2
    chunks, chunk = v_pair.shape[0], v_pair.shape[-1]
    partner = (o, 2 * q + 1 - c)
    side = (2 * z + 1 - low, s)

    def cols(k):
        return pl.ds(k * chunk, chunk)

    def v_swap(k):
        return remote(vir.at[:, :, 1 - c, :, cols(k)], v_pair.at[k], vp_send.at[k], vp_recv.at[k], partner)

    def x_swap(k):
        return remote(v_sum.at[k, :, 1 - low], v_side.at[k], x_send.at[k], x_recv.at[k], side)

    def along(k, d):
        there = (z + d) % nz
        return remote(
            v_line.at[k, there], v_chain.at[k, d], z_send.at[k, d], z_recv.at[k, d], (2 * there + low, s)
        )

    def between(k, d):
        there = (q + d) % nq
        return remote(v_col.at[k, there], v_far.at[k, d], y_send.at[k, d], y_recv.at[k, d], (o, 2 * there + c))

    def swap(d):
        return remote(three.at[(q + d) % nq, 1 - c], t_pair.at[d], pair_send.at[d], pair_recv.at[d], partner)

    def spread(d):
        return remote(t_out.at[d], t_far.at[d], t_send.at[d], t_recv.at[d], (o, 2 * ((q + d) % nq) + c))

    order = list(range(1, nq)) + [0]

    def open_vir():
        for k in range(chunks):
            v_swap(k).start()

    def close():
        for d in order:
            swap(d).start()
        for k in range(chunks):
            v_swap(k).wait()
            v_sum[k] = (vir[:, :, c, :, cols(k)] + v_pair[k]).reshape(v_sum.shape[1:])
            x_swap(k).start()
        for d in order[:-1]:
            swap(d).wait()
            t_out[d] = three[(q + d) % nq, c] + t_pair[d]
            spread(d).start()
        for k in range(chunks):
            x_swap(k).wait()
            v_line[k] = v_sum[k, :, low] + v_side[k]
            for d in range(1, nz):
                along(k, d).start()
            if k == 0:
                swap(0).wait()
                near_out[...] = three[q, c] + t_pair[0]
        for k in range(chunks):
            held = v_line[k, z]
            for d in range(1, nz):
                along(k, d).wait()
                held += v_chain[k, d]
            v_col[k] = held
            for d in range(1, nq):
                between(k, d).start()
        for d in order[:-1]:
            spread(d).wait()
            far_out[...] = t_far[d] if d == 1 else far_out[...] + t_far[d]
        for k in range(chunks):
            rows = v_col[k, q]
            for d in range(1, nq):
                between(k, d).wait()
                rows += v_far[k, d]
            vir_out[:, cols(k)] = rows

    return open_vir, close


def amplitude_kernel(n, nq, *refs):
    make_densities(n, nq, *refs)()


def reduce_kernel(n, nq, *refs):
    greet(n, nq)()
    open_vir, close = reduction(n, nq, *refs)
    open_vir()
    close()


def whole_kernel(n, nq, inputs, outputs, count, *refs):
    operands, results, scratch = refs[:inputs], refs[inputs : inputs + outputs], refs[inputs + outputs :]
    three, vir, rest = scratch[0], scratch[1], scratch[2:]
    open_vir, close = reduction(n, nq, three, vir, *results, *rest[count:])
    finish = make_densities(n, nq, *operands, three, vir, *rest[:count], vir_done=open_vir)
    close()
    finish()


def per_device(half_integrals, vir_coef, occ_energy, vir_energy):
    n, aux = lax.axis_size("occ"), lax.axis_size("aux")
    nz, nq = n // 2, aux // 2
    _, tile, basis = half_integrals.shape
    part = vir_coef.shape[1]
    virtuals = part * n
    width, rows = virtuals // aux, virtuals // (n * aux)
    vmem = pl.BlockSpec(memory_space=pltpu.VMEM)
    dma = pltpu.SemaphoreType.DMA
    half = jnp.bfloat16
    lanes = 128
    chunks = virtuals // lanes

    def room(*shape):
        return pltpu.VMEM(shape, F32)

    def result(*shape):
        return jax.ShapeDtypeStruct(shape, F32)

    def call(kernel, name, number, in_specs, out_shape, scratch, operands):
        return pl.pallas_call(
            kernel,
            out_shape=out_shape,
            in_specs=in_specs,
            out_specs=(vmem,) * len(out_shape),
            scratch_shapes=scratch,
            compiler_params=pltpu.CompilerParams(
                collective_id=number, has_side_effects=True, vmem_limit_bytes=LIMIT
            ),
            name=name,
        )(*operands)

    operands = (occ_energy, half_integrals, vir_coef.T, vir_energy)
    specs = [pl.BlockSpec(memory_space=pltpu.SMEM), pl.BlockSpec(memory_space=pl.ANY), vmem, vmem]
    make_scratch = [
        pltpu.VMEM(half_integrals.shape, half),
        pltpu.VMEM((2, virtuals, basis // 2), half),
        pltpu.VMEM((nq, 2, nq, 2 * width, tile), half),
        pltpu.VMEM((nq, 2, n * width, tile), half),
        pltpu.VMEM((n, width, tile), half),
        pltpu.VMEM((n * width, virtuals), half),
        dma, dma((2,)), dma, dma((n,)), dma((nz,)), dma((nz,)), dma((nz,)), dma((n,)), dma((n,)),
        dma((nq, nq)), dma((nq, nq)), dma((nq, nq)), dma((nq, nq)), dma((nq,)), dma((nq,)), dma((n,)), dma((n,)),
        dma((nq, n)), dma((nq, nz)), dma((nq, nz)), dma((nq, nz)),
    ]
    reduce_scratch = [
        room(nq, tile, virtuals), room(nq, tile, virtuals), room(nq, tile, virtuals),
        room(chunks, n, nq, rows, lanes), room(chunks, nz, 2, nq, rows, lanes),
        room(chunks, nz, nq, rows, lanes), room(chunks, nz, nq, rows, lanes), room(chunks, nz, nq, rows, lanes),
        room(chunks, nq, rows, lanes), room(chunks, nq, rows, lanes),
        dma((nq,)), dma((nq,)), dma((nq,)), dma((nq,)), dma((chunks,)), dma((chunks,)), dma((chunks,)), dma((chunks,)),
        dma((chunks, nz)), dma((chunks, nz)), dma((chunks, nq)), dma((chunks, nq)),
    ]
    sums = (nq, 2, tile, virtuals)
    groups = (n, nq, 2, rows, virtuals)
    finals = (result(tile, virtuals), result(tile, virtuals), result(rows, virtuals))
    if rows % 8 == 0:
        kernel = functools.partial(whole_kernel, n, nq, len(specs), len(finals), len(make_scratch))
        scratch = [room(*sums), room(*groups)] + make_scratch + reduce_scratch
        near, far, vir_rows = call(kernel, "densities", 0, specs, finals, scratch, operands)
    else:
        kernel = functools.partial(amplitude_kernel, n, nq)
        partials = (result(*sums), result(virtuals, virtuals))
        three, vir = call(kernel, "amplitude", 0, specs, partials, make_scratch, operands)
        kernel = functools.partial(reduce_kernel, n, nq)
        near, far, vir_rows = call(
            kernel, "reduce", 1, [vmem, vmem], finals, reduce_scratch, (three, vir.reshape(groups))
        )
    return (near + far)[:, None, :], vir_rows / (n * virtuals)


def solution(mesh):
    return jax.shard_map(
        per_device,
        mesh=mesh,
        in_specs=(P(None, "aux", None), P(None, "occ"), P(), P()),
        out_specs=(P("aux", "occ", None), P(("occ", "aux"), None)),
        check_vma=False,
    )
```
